128 devices in a mesh: row: 16 (over y, x), col: 8 (over z, core).
Axes of the slice: x: 4, y: 4, z: 4, core: 2. Of those that a mesh axis runs over, the one named last changes fastest.
Arguments:
- orbitals: float32 [32768, 1024], P('row', 'col'), may hold values from -6 to 6
- point_index: int32 [8192], replicated, may hold values from 0 to 32767, as said below
- coulomb: float32 [8192, 8192], P('row', 'col'), may hold values from -0.001953125 to 0.001953125
- fitting: float32 [32768, 8192], P('row', 'col'), may hold values from -0.0625 to 0.0625
Outputs:
- exchange_out: float32 [32768, 1024], P('row', 'col')
The draws below stay inside these ranges and needn't reach their ends.
Inputs may be any that keep to these rules, and one draw needn't show every extreme that they name: `point_index`: indices are distinct. Grid index g lies in slab g // 2048. Of the 512 consecutive points of each row panel, at most 64 lie in one slab, and in every panel exactly 64 lie in one slab.
All inputs are finite; a program needn't handle non-finite values.
Results may differ from the reference program's by a relative error of at most 0.00012.
Values sent between devices are 32-bit elements; how exact they have to be, the bound alone decides.
No kernel may reach another device: no remote copies, remote signals or barrier semaphores. Data moves between devices by JAX's collectives and lax.ppermute only.
A program may use at most 64 MiB of HBM per device.

```python
import jax
import jax.numpy as jnp
from jax import lax

NB = 1024
P_SIZE = 8192
GS = 2048
G = 32768
PANEL = 512
SLOT = 64
N_ROW = 16


def draw_point_index(key, part):
    key_slab = jax.random.fold_in(key, 11)
    key_shuffle = jax.random.fold_in(key, 23)
    key_rows = jax.random.fold_in(key, 37)
    slab_perms = jax.vmap(lambda k: jax.random.permutation(k, N_ROW))(jax.random.split(key_slab, N_ROW))
    position = jnp.arange(PANEL)
    which = jnp.where(position < SLOT, 0, 1 + (position - SLOT) % (N_ROW - 1))
    owners = slab_perms[:, which]
    owners = jax.vmap(lambda k, o: jax.random.permutation(k, o))(jax.random.split(key_shuffle, N_ROW), owners)
    owner_flat = owners.reshape(-1).astype(jnp.int32)
    onehot = (owner_flat[:, None] == jnp.arange(N_ROW)[None, :]).astype(jnp.int32)
    ranks = jnp.sum(jnp.where(onehot > 0, jnp.cumsum(onehot, axis=0) - 1, 0), axis=1)
    row_perms = jax.vmap(lambda k: jax.random.permutation(k, GS))(jax.random.split(key_rows, N_ROW))
    local = row_perms[owner_flat, ranks]
    return (owner_flat * GS + local).astype(jnp.int32)


def levels(own_key, extent, cuts, smallest, top_value):
    def one(dim, blocks):
        draws = jax.random.uniform(jax.random.fold_in(jax.random.fold_in(own_key, 6), dim), (blocks,), jnp.float32, smallest / len(cuts), top_value / len(cuts))
        return jnp.repeat(jnp.exp(draws), extent[dim] // blocks).reshape((-1,) + (1,) * (len(extent) - dim - 1))

    loudness = one(*cuts[0])
    for cut in cuts[1:]:
        loudness = loudness * one(*cut)
    return loudness


def scatter_about(rng, extent, spread, bound, shards=(), dtype=jnp.bfloat16):
    array = spread * jax.random.normal(rng, extent, jnp.float32)
    if shards:
        array = array * levels(rng, extent, shards, -0.22, 0.18)
    return jnp.clip(array, -bound, bound).astype(dtype)


def setup_inputs(seed: int = 0) -> dict:
    seeds = jax.random.split(jax.random.key(seed), 5)
    return {
        "orbitals": scatter_about(seeds[0], (G, NB), 1.0, 6.0, ((0, 16), (1, 8)), jnp.float32),
        "point_index": draw_point_index(jax.random.fold_in(seeds[4], 71), 0),
        "coulomb": scatter_about(seeds[2], (P_SIZE, P_SIZE), (P_SIZE * NB) ** -0.5, 0.001953125, ((0, 16), (1, 8)), jnp.float32),
        "fitting": scatter_about(seeds[3], (G, P_SIZE), P_SIZE ** -0.5, 0.0625, ((0, 16), (1, 8)), jnp.float32),
    }


def reference(orbitals, point_index, coulomb, fitting):
    picked = orbitals[point_index]
    pair = jnp.dot(picked, picked.T, precision=lax.Precision.HIGHEST, preferred_element_type=jnp.float32)
    weights = jnp.dot(coulomb * pair, picked, precision=lax.Precision.HIGHEST, preferred_element_type=jnp.float32)
    return -jnp.dot(fitting, weights, precision=lax.Precision.HIGHEST, preferred_element_type=jnp.float32)
```

```python
import functools

import jax
import jax.numpy as jnp
from jax import lax
from jax.experimental import pallas as pl
from jax.experimental.pallas import tpu as pltpu
from jax.sharding import PartitionSpec as P


SIDE = 4
REL = (0, -1, 1, 2)
F32 = jnp.float32
BF16 = jnp.bfloat16


def shift(axis, step):
    pairs = []
    if axis == "z":
        for z in range(SIDE):
            for k in range(2):
                pairs.append((z * 2 + k, ((z + step) % SIDE) * 2 + k))
        return "col", pairs
    for y in range(SIDE):
        for x in range(SIDE):
            ty = (y + step) % SIDE if axis == "y" else y
            tx = (x + step) % SIDE if axis == "x" else x
            pairs.append((y * SIDE + x, ty * SIDE + tx))
    return "row", pairs


def move(value, axis, step):
    name, pairs = shift(axis, step)
    return lax.ppermute(value, name, pairs)


def swap_cores(value):
    return lax.ppermute(value, "col", [(c, c ^ 1) for c in range(2 * SIDE)])


def scatter_pairs(turn):
    pairs = []
    for y in range(SIDE):
        for x in range(SIDE):
            for z in range(SIDE):
                for k in range(2):
                    strip = (z + turn) % SIDE
                    ty = (strip - y) % SIDE
                    tx = x if k == 0 else x ^ 3
                    target = (ty * SIDE + tx) * 8 + y * 2 + (x >> 1)
                    pairs.append(((y * SIDE + x) * 8 + z * 2 + k, target))
    return pairs


def to_plane(value, turn):
    return lax.ppermute(value, ("row", "col"), scatter_pairs(turn))


def gather_line(block, axis):
    half = block.shape[0] // 2
    before = move(block, axis, 1)
    after = move(block, axis, -1)
    far_low = move(before[:half], axis, 1)
    far_high = move(after[half:], axis, -1)
    return block, before, after, far_low, far_high


def gather_plane(block):
    half = block.shape[0] // 2
    first = gather_line(block[:half], "x")
    second = gather_line(block[half:], "y")
    shape = (SIDE, half) + block.shape[1:]
    first = jnp.concatenate(first, axis=0).reshape(shape)
    second = jnp.concatenate(second, axis=0).reshape(shape)
    return gather_line(first, "y") + gather_line(second, "x")


def plane_order(my_row, my_col):
    rel = jnp.array(REL, jnp.int32)
    y, x = my_row // SIDE, my_row % SIDE
    z, k = my_col // 2, my_col % 2
    outer, inner = jnp.repeat(rel, SIDE), jnp.tile(rel, SIDE)

    def describe(dy, dx):
        py, px = (y + dy) % SIDE, (x + dx) % SIDE
        strip_k = (px >> 1) ^ k
        panel = (px & 1) ^ strip_k
        return panel, ((py + z) % SIDE) * 2 + strip_k

    first, second = describe(outer, inner), describe(inner, outer)
    return jnp.stack([first[0], first[1], second[0], second[1]])


def split(value):
    high = value.astype(BF16)
    return high, (value - high.astype(F32)).astype(BF16)


def dot3(a_high, a_low, b_high, b_low, dims):
    dot = functools.partial(
        lax.dot_general, dimension_numbers=(dims, ((), ())), preferred_element_type=F32
    )
    return dot(a_high, b_high) + (dot(a_high, b_low) + dot(a_low, b_high))


def piece_blocks(pieces):
    found, position = [], 0
    for ref in pieces:
        for block in range(ref.shape[0]):
            found.append((ref, block, position))
            position += 1
    return found


def pair_kernel(order, panel_order, *refs):
    first, second, panels = refs[:5], refs[5:10], refs[10:15]
    coulomb, keep, send = refs[15:18]
    column, panel, p_high, p_low, total, column_sem, panel_sem = refs[18:]
    rows = first[0].shape[1]
    lanes = first[0].shape[2]
    panel_copies = []
    for ref, block, position in piece_blocks(panels):
        lane = pl.multiple_of(panel_order[position] * lanes, lanes)
        panel_copies.append(
            pltpu.make_async_copy(ref.at[block], panel.at[:, pl.ds(lane, lanes)], panel_sem.at[position])
        )
        panel_copies[-1].start()
    for which, pieces in enumerate((first, second)):
        for ref, block, position in piece_blocks(pieces):
            part = order[2 * which, position] * 2 + which
            strip = order[2 * which + 1, position]
            row = pl.multiple_of(part * rows, rows)
            lane = pl.multiple_of(strip * lanes, lanes)
            pltpu.make_async_copy(
                ref.at[block],
                column.at[pl.ds(row, rows), pl.ds(lane, lanes)],
                column_sem.at[part * 8 + strip],
            ).start()
    for copy in panel_copies:
        copy.wait()
    p_high[...], p_low[...] = split(panel[...])
    total[...] = jnp.zeros_like(total)

    @pl.loop(0, 4)
    def _(step):
        part = lax.rem(step, 2) * 2 + step // 2
        here = pl.ds(pl.multiple_of(part * rows, rows), rows)
        for strip in range(8):
            pltpu.make_async_copy(
                first[0].at[0], column.at[here, pl.ds(strip * lanes, lanes)], column_sem.at[part * 8 + strip]
            ).wait()
        high, low = split(column[here, :])
        pair = dot3(p_high[...], p_low[...], high, low, ((1,), (1,)))
        t_high, t_low = split(coulomb[:, here] * pair)
        total[...] += dot3(t_high, t_low, high, low, ((1,), (0,)))

    core, height = panel_order[8], panel_order[9]
    count = keep.shape[1]
    for turn in range(SIDE):
        strip = lax.rem(height + turn, SIDE) * 2
        keep[turn] = total[pl.ds(pl.multiple_of((strip + core) * count, count), count), :]
        send[turn] = total[pl.ds(pl.multiple_of((strip + 1 - core) * count, count), count), :]


def pair_weights(order, panel_order, column_pieces, panel_pieces, coulomb):
    rows, width = coulomb.shape
    bands = 8 * 128
    anywhere = pl.BlockSpec(memory_space=pl.ANY)
    scalars = pl.BlockSpec(memory_space=pltpu.SMEM)
    vmem = pl.BlockSpec(memory_space=pltpu.VMEM)
    out = jax.ShapeDtypeStruct((SIDE, rows // 8, bands), F32)
    return pl.pallas_call(
        pair_kernel,
        out_shape=(out, out),
        in_specs=[scalars, scalars] + [anywhere] * 15 + [vmem],
        out_specs=(vmem, vmem),
        scratch_shapes=[
            pltpu.VMEM((width, bands), F32),
            pltpu.VMEM((rows, bands), F32),
            pltpu.VMEM((rows, bands), BF16),
            pltpu.VMEM((rows, bands), BF16),
            pltpu.VMEM((rows, bands), F32),
            pltpu.SemaphoreType.DMA((32,)),
            pltpu.SemaphoreType.DMA((8,)),
        ],
        compiler_params=pltpu.CompilerParams(vmem_limit_bytes=26 << 20),
        cost_estimate=pl.CostEstimate(flops=12 * rows * width * bands, bytes_accessed=12 << 20, transcendentals=0),
        name="pair_weights",
    )(order, panel_order, *column_pieces, *panel_pieces, coulomb)


def term_kernel(groups, gathered, where, *refs):
    refs = list(refs)
    if gathered:
        order, first, second = refs[0], refs[1:6], refs[6:11]
        refs = refs[11:]
        outs, (high, low, whole, sem) = refs[1:-4], refs[-4:]

        @pl.when(pl.program_id(0) == 0)
        def _():
            rows = first[0].shape[1]
            copies = []
            for which, pieces in enumerate((first, second)):
                for ref, block, position in piece_blocks(pieces):
                    strip = order[2 * which, position] * 8 + order[2 * which + 1, position]
                    row = pl.multiple_of((strip * 2 + which) * rows, rows)
                    copies.append(
                        pltpu.make_async_copy(
                            ref.at[block], whole.at[pl.ds(row, rows), :], sem.at[which * 16 + position]
                        )
                    )
            for copy in copies:
                copy.start()
            for copy in copies:
                copy.wait()
            high[...], low[...] = split(whole[...])
    else:
        weights, outs = refs[1 : 1 + 2 * groups], refs[2 + 2 * groups :]
    f_high, f_low = split(refs[0][...])
    even = where[SIDE] == 0
    half = outs[0].shape[1]
    bands = 2 * half
    for group in range(groups):
        if gathered:
            here = pl.ds(pl.multiple_of(where[group] * bands, bands), bands)
            w_high, w_low = high[:, here], low[:, here]
        else:
            w_high, w_low = weights[2 * group][...], weights[2 * group + 1][...]
        product = dot3(f_high, f_low, w_high, w_low, ((1,), (0,)))
        lower, upper = product[:, :half], product[:, half:]
        outs[2 * group][...] = jnp.where(even, lower, upper)
        outs[2 * group + 1][...] = jnp.where(even, upper, lower)


def term(groups, where, fitting, weights=None, after=None, order=None, pieces=None):
    rows, points = fitting.shape
    bands = 8 * 128
    tile = 512
    gathered = pieces is not None
    halves = 2 * groups
    anywhere = pl.BlockSpec(memory_space=pltpu.HBM)
    streamed = pl.BlockSpec((tile, points), lambda i, where: (i, 0))
    resident = pl.BlockSpec((points, bands), lambda i, where: (0, 0), pipeline_mode=pl.Buffered(1))
    half = pl.BlockSpec((tile, bands // 8), lambda i, where: (i, 0))
    out = [jax.ShapeDtypeStruct((rows, bands // 8), F32)] * halves
    out_specs = [half] * halves
    scratch = []
    if gathered:
        in_specs = [pl.BlockSpec(memory_space=pltpu.SMEM)] + [anywhere] * 10 + [streamed]
        operands = (order, *pieces, fitting)
        out += [jax.ShapeDtypeStruct((points, bands), BF16)] * 2
        out_specs += [resident] * 2
        scratch = [pltpu.VMEM((points, bands), F32), pltpu.SemaphoreType.DMA((32,))]
    else:
        in_specs, operands = [streamed], [fitting]
        for group in range(groups):
            chosen = pl.BlockSpec((points, bands // SIDE), lambda i, where, group=group: (0, where[group]))
            in_specs += [chosen, chosen]
            operands += weights
        in_specs.append(anywhere)
        operands.append(after)
    return pl.pallas_call(
        functools.partial(term_kernel, groups, gathered),
        out_shape=out,
        grid_spec=pltpu.PrefetchScalarGridSpec(
            num_scalar_prefetch=1,
            grid=(rows // tile,),
            in_specs=in_specs,
            out_specs=out_specs,
            scratch_shapes=scratch,
        ),
        cost_estimate=pl.CostEstimate(
            flops=6 * groups * rows * points * bands // SIDE, bytes_accessed=11 << 20, transcendentals=0
        ),
        name="term",
    )(where, *operands)


def picked_strip(orbitals, point_index, my_row):
    row_count = SIDE * SIDE
    slab_rows, lanes = orbitals.shape
    per_panel = point_index.shape[0] // row_count
    slot_count = 2 * per_panel // row_count
    owner = point_index // slab_rows
    owner_grid = owner.reshape(row_count, per_panel)
    local_grid = (point_index - owner * slab_rows).reshape(row_count, per_panel)
    spot = jnp.arange(per_panel)
    earlier = (spot[:, None] < spot[None, :]).astype(BF16)
    mine = owner_grid == my_row
    rank = jnp.dot(mine.astype(BF16), earlier, preferred_element_type=F32).astype(jnp.int32)
    chosen = mine[:, :, None] & (rank[:, :, None] == jnp.arange(slot_count)[None, None, :])
    source_row = jnp.sum(jnp.where(chosen, local_grid[:, :, None], 0), axis=1)
    outgoing = orbitals[source_row.reshape(-1)].reshape(row_count, slot_count, lanes)
    received = lax.all_to_all(outgoing, "row", split_axis=0, concat_axis=0, tiled=True)
    owner_mine = lax.dynamic_slice_in_dim(owner_grid, my_row, 1, 0)[0]
    matches = owner_mine[None, :] == jnp.arange(row_count)[:, None]
    ranks = jnp.dot(matches.astype(BF16), earlier, preferred_element_type=F32).astype(jnp.int32)
    slot_mine = jnp.sum(jnp.where(matches, ranks, 0), axis=0)
    return received.reshape(row_count * slot_count, lanes)[owner_mine * slot_count + slot_mine]


def exchange(orbitals, point_index, coulomb, fitting):
    my_row = lax.axis_index("row")
    my_col = lax.axis_index("col")
    height, core = my_col // 2, my_col % 2
    order = plane_order(my_row, my_col)
    strip = picked_strip(orbitals, point_index, my_row)

    column_pieces = gather_plane(to_plane(strip, 0))
    both = jnp.stack([strip, swap_cores(strip)])
    before, after = move(both, "z", 1), move(both, "z", -1)
    panel_pieces = (both, before, after, move(before[:1], "z", 1), move(after[1:], "z", -1))
    place = jnp.array(REL, jnp.int32).repeat(2)
    cores = jnp.tile(jnp.array([0, 1], jnp.int32), SIDE)
    panel_order = jnp.concatenate(
        [((height + place) % SIDE) * 2 + (core ^ cores), jnp.stack([core, height])]
    ).astype(jnp.int32)
    keep, send = pair_weights(order, panel_order, column_pieces, panel_pieces, coulomb)

    summed = keep + swap_cores(send)
    parts = [to_plane(summed[turn], turn) for turn in range(SIDE)]
    w_strip = (parts[0] + parts[1]) + (parts[2] + parts[3])
    pieces = gather_plane(w_strip)

    def targets(*steps):
        chips = [(height + step) % SIDE for step in steps] + [height] * (SIDE - len(steps))
        return jnp.stack(chips + [core]).astype(jnp.int32)

    half = fitting.shape[0] // 2
    mine, other, *weights = term(1, targets(2), fitting, order=order, pieces=pieces)
    far = mine + swap_cores(other)
    far_up = move(far[:half], "z", 1)
    far_down = move(far[half:], "z", -1)
    chips, tag = targets(1, -1), far[:8]
    mine, other, mine_down, other_down = term(2, chips, fitting, weights, tag)
    up = mine + swap_cores(other)
    down = mine_down + swap_cores(other_down)
    up_high = move(up[half:], "z", 1)
    down_low = move(down[:half], "z", -1)
    up_low = move(up[:half] + far_up, "z", 1)
    down_high = move(down[half:] + far_down, "z", -1)
    chips, tag = targets(0), up[:8] + down[:8]
    mine, other = term(1, chips, fitting, weights, tag)
    own = mine + swap_cores(other)
    low = own[:half] + (up_low + down_low)
    high = own[half:] + (up_high + down_high)
    return -jnp.concatenate([low, high], axis=0)


def solution(mesh):
    in_specs = (P("row", "col"), P(), P("row", "col"), P("row", "col"))
    out_specs = P("row", "col")
    return jax.shard_map(exchange, mesh=mesh, in_specs=in_specs, out_specs=out_specs, check_vma=False)
```

```python
import functools

import jax
import jax.numpy as jnp
from jax import lax
from jax.experimental import pallas as pl
from jax.experimental.pallas import tpu as pltpu
from jax.sharding import PartitionSpec as P


SIDE = 4
REL = (0, -1, 1, 2)
F32 = jnp.float32
BF16 = jnp.bfloat16


def shift(axis, step):
    pairs = []
    if axis == "z":
        for z in range(SIDE):
            for k in range(2):
                pairs.append((z * 2 + k, ((z + step) % SIDE) * 2 + k))
        return "col", pairs
    for y in range(SIDE):
        for x in range(SIDE):
            ty = (y + step) % SIDE if axis == "y" else y
            tx = (x + step) % SIDE if axis == "x" else x
            pairs.append((y * SIDE + x, ty * SIDE + tx))
    return "row", pairs


def move(value, axis, step):
    name, pairs = shift(axis, step)
    return lax.ppermute(value, name, pairs)


def swap_cores(value):
    return lax.ppermute(value, "col", [(c, c ^ 1) for c in range(2 * SIDE)])


def scatter_pairs(turn):
    pairs = []
    for y in range(SIDE):
        for x in range(SIDE):
            for z in range(SIDE):
                for k in range(2):
                    strip = (z + turn) % SIDE
                    ty = (strip - y) % SIDE
                    tx = x if k == 0 else x ^ 3
                    target = (ty * SIDE + tx) * 8 + y * 2 + (x >> 1)
                    pairs.append(((y * SIDE + x) * 8 + z * 2 + k, target))
    return pairs


def to_plane(value, turn):
    return lax.ppermute(value, ("row", "col"), scatter_pairs(turn))


def gather_line(low, high, axis):
    before_low, after_high = move(low, axis, 1), move(high, axis, -1)
    before_high, after_low = move(high, axis, 1), move(low, axis, -1)
    far_low, far_high = move(before_low, axis, 1), move(after_high, axis, -1)
    return low, high, before_low, before_high, after_low, after_high, far_low, far_high


def line_halves(block, axis):
    before, after, far = move(block, axis, 1), move(block, axis, -1), move(block, axis, 2)
    return jnp.stack([block, before]), jnp.stack([after, far])


def gather_plane(block):
    half = block.shape[0] // 2
    first = line_halves(block[:half], "x")
    second = line_halves(block[half:], "y")
    return gather_line(*first, "y") + gather_line(*second, "x")


def plane_order(my_row, my_col):
    rel = jnp.array(REL, jnp.int32)
    y, x = my_row // SIDE, my_row % SIDE
    z, k = my_col // 2, my_col % 2
    outer, inner = jnp.repeat(rel, SIDE), jnp.tile(rel, SIDE)

    def describe(dy, dx):
        py, px = (y + dy) % SIDE, (x + dx) % SIDE
        strip_k = (px >> 1) ^ k
        panel = (px & 1) ^ strip_k
        return panel, ((py + z) % SIDE) * 2 + strip_k

    first, second = describe(outer, inner), describe(inner, outer)
    return jnp.stack([first[0], first[1], second[0], second[1]])


def split(value):
    high = value.astype(BF16)
    return high, (value - high.astype(F32)).astype(BF16)


def dot3(a_high, a_low, b_high, b_low, dims):
    dot = functools.partial(
        lax.dot_general, dimension_numbers=(dims, ((), ())), preferred_element_type=F32
    )
    return dot(a_high, b_high) + (dot(a_high, b_low) + dot(a_low, b_high))


def piece_blocks(pieces):
    found, position = [], 0
    for ref in pieces:
        for block in range(ref.shape[0]):
            found.append((ref, block, position))
            position += 1
    return found


def pair_kernel(order, panel_order, *refs):
    first, second, panels = refs[:8], refs[8:16], refs[16:24]
    coulomb, keep, send = refs[24:27]
    column, panel, p_high, p_low, total, column_sem, panel_sem = refs[27:]
    rows = first[0].shape[1]
    lanes = first[0].shape[2]
    panel_copies = []
    for ref, block, position in piece_blocks(panels):
        lane = pl.multiple_of(panel_order[position] * lanes, lanes)
        panel_copies.append(
            pltpu.make_async_copy(ref.at[block], panel.at[:, pl.ds(lane, lanes)], panel_sem.at[position])
        )
        panel_copies[-1].start()
    for which, pieces in enumerate((first, second)):
        for ref, block, position in piece_blocks(pieces):
            part = order[2 * which, position] * 2 + which
            strip = order[2 * which + 1, position]
            row = pl.multiple_of(part * rows, rows)
            lane = pl.multiple_of(strip * lanes, lanes)
            pltpu.make_async_copy(
                ref.at[block],
                column.at[pl.ds(row, rows), pl.ds(lane, lanes)],
                column_sem.at[part * 8 + strip],
            ).start()
    for copy in panel_copies:
        copy.wait()
    p_high[...], p_low[...] = split(panel[...])
    total[...] = jnp.zeros_like(total)

    @pl.loop(0, 4)
    def _(step):
        part = lax.rem(step, 2) * 2 + step // 2
        here = pl.ds(pl.multiple_of(part * rows, rows), rows)
        for strip in range(8):
            pltpu.make_async_copy(
                first[0].at[0], column.at[here, pl.ds(strip * lanes, lanes)], column_sem.at[part * 8 + strip]
            ).wait()
        high, low = split(column[here, :])
        pair = dot3(p_high[...], p_low[...], high, low, ((1,), (1,)))
        t_high, t_low = split(coulomb[:, here] * pair)
        total[...] += dot3(t_high, t_low, high, low, ((1,), (0,)))

    core, height = panel_order[8], panel_order[9]
    count = keep.shape[1]
    for turn in range(SIDE):
        strip = lax.rem(height + turn, SIDE) * 2
        keep[turn] = total[pl.ds(pl.multiple_of((strip + core) * count, count), count), :]
        send[turn] = total[pl.ds(pl.multiple_of((strip + 1 - core) * count, count), count), :]


def pair_weights(order, panel_order, column_pieces, panel_pieces, coulomb):
    rows, width = coulomb.shape
    bands = 8 * 128
    anywhere = pl.BlockSpec(memory_space=pl.ANY)
    scalars = pl.BlockSpec(memory_space=pltpu.SMEM)
    vmem = pl.BlockSpec(memory_space=pltpu.VMEM)
    out = jax.ShapeDtypeStruct((SIDE, rows // 8, bands), F32)
    return pl.pallas_call(
        pair_kernel,
        out_shape=(out, out),
        in_specs=[scalars, scalars] + [anywhere] * 24 + [vmem],
        out_specs=(vmem, vmem),
        scratch_shapes=[
            pltpu.VMEM((width, bands), F32),
            pltpu.VMEM((rows, bands), F32),
            pltpu.VMEM((rows, bands), BF16),
            pltpu.VMEM((rows, bands), BF16),
            pltpu.VMEM((rows, bands), F32),
            pltpu.SemaphoreType.DMA((32,)),
            pltpu.SemaphoreType.DMA((8,)),
        ],
        compiler_params=pltpu.CompilerParams(vmem_limit_bytes=26 << 20),
        cost_estimate=pl.CostEstimate(flops=12 * rows * width * bands, bytes_accessed=12 << 20, transcendentals=0),
        name="pair_weights",
    )(order, panel_order, *column_pieces, *panel_pieces, coulomb)


def term_kernel(gathered, where, *refs):
    tile = pl.program_id(0)
    if gathered:
        order, first, second = refs[0], refs[1:9], refs[9:17]
        fitting, outs, (high, low, whole, sem) = refs[17], refs[18:22], refs[22:]

        @pl.when(tile == 0)
        def _():
            rows = first[0].shape[1]
            copies = []
            for which, pieces in enumerate((first, second)):
                for ref, block, position in piece_blocks(pieces):
                    strip = order[2 * which, position] * 8 + order[2 * which + 1, position]
                    row = pl.multiple_of((strip * 2 + which) * rows, rows)
                    copies.append(
                        pltpu.make_async_copy(
                            ref.at[block], whole.at[pl.ds(row, rows), :], sem.at[which * 16 + position]
                        )
                    )
            for copy in copies:
                copy.start()
            for copy in copies:
                copy.wait()
            high[...], low[...] = split(whole[...])
    else:
        fitting, weights, outs = refs[0], refs[1:5], refs[7:11]
    f_high, f_low = split(fitting[...])
    even = where[3] == 0
    half = outs[0].shape[2]
    for group in range(2):
        if gathered:
            start = chip_of(group, tile, where) * 2 * half
            here = pl.ds(pl.multiple_of(start, 2 * half), 2 * half)
            w_high, w_low = high[:, here], low[:, here]
        else:
            w_high, w_low = weights[2 * group][...], weights[2 * group + 1][...]
        product = dot3(f_high, f_low, w_high, w_low, ((1,), (0,)))
        lower, upper = product[:, :half], product[:, half:]
        outs[2 * group][0] = jnp.where(even, lower, upper)
        outs[2 * group + 1][0] = jnp.where(even, upper, lower)


def chip_of(group, tile, where):
    return where[0] if group == 0 else jnp.where(tile < 2, where[1], where[2])


def term(where, fitting, gathered=None, weights=None, after=None):
    rows, points = fitting.shape
    bands = 8 * 128
    tile = rows // 4
    anywhere = pl.BlockSpec(memory_space=pltpu.HBM)
    streamed = pl.BlockSpec((tile, points), lambda i, where: (i, 0))
    resident = pl.BlockSpec((points, bands), lambda i, where: (0, 0), pipeline_mode=pl.Buffered(1))
    half = pl.BlockSpec((1, tile, bands // 8), lambda i, where: (i // 2, lax.rem(i, 2), 0))
    out = [jax.ShapeDtypeStruct((2, rows // 2, bands // 8), F32)] * 4
    out_specs = [half] * 4
    scratch = []
    if gathered is not None:
        in_specs = [pl.BlockSpec(memory_space=pltpu.SMEM)] + [anywhere] * 16 + [streamed]
        operands = (*gathered, fitting)
        out += [jax.ShapeDtypeStruct((points, bands), BF16)] * 2
        out_specs += [resident] * 2
        scratch = [pltpu.VMEM((points, bands), F32), pltpu.SemaphoreType.DMA((32,))]
    else:
        in_specs = [streamed]
        for group in range(2):
            chosen = pl.BlockSpec(
                (points, bands // SIDE), lambda i, where, group=group: (0, chip_of(group, i, where))
            )
            in_specs += [chosen, chosen]
        in_specs += [anywhere] * 2
        operands = (fitting, *weights, *weights, *after)
    return pl.pallas_call(
        functools.partial(term_kernel, gathered is not None),
        out_shape=out,
        grid_spec=pltpu.PrefetchScalarGridSpec(
            num_scalar_prefetch=1,
            grid=(rows // tile,),
            in_specs=in_specs,
            out_specs=out_specs,
            scratch_shapes=scratch,
        ),
        cost_estimate=pl.CostEstimate(
            flops=12 * rows * points * bands // SIDE, bytes_accessed=16 << 20, transcendentals=0
        ),
        name="term",
    )(where, *operands)


def picked_strip(orbitals, point_index, my_row):
    row_count = SIDE * SIDE
    slab_rows, lanes = orbitals.shape
    per_panel = point_index.shape[0] // row_count
    slot_count = 2 * per_panel // row_count
    owner = point_index // slab_rows
    owner_grid = owner.reshape(row_count, per_panel)
    local_grid = (point_index - owner * slab_rows).reshape(row_count, per_panel)
    spot = jnp.arange(per_panel)
    earlier = (spot[:, None] < spot[None, :]).astype(BF16)
    mine = owner_grid == my_row
    rank = jnp.dot(mine.astype(BF16), earlier, preferred_element_type=F32).astype(jnp.int32)
    chosen = mine[:, :, None] & (rank[:, :, None] == jnp.arange(slot_count)[None, None, :])
    source_row = jnp.sum(jnp.where(chosen, local_grid[:, :, None], 0), axis=1)
    outgoing = orbitals[source_row.reshape(-1)].reshape(row_count, slot_count, lanes)
    received = lax.all_to_all(outgoing, "row", split_axis=0, concat_axis=0, tiled=True)
    owner_mine = lax.dynamic_slice_in_dim(owner_grid, my_row, 1, 0)[0]
    matches = owner_mine[None, :] == jnp.arange(row_count)[:, None]
    ranks = jnp.dot(matches.astype(BF16), earlier, preferred_element_type=F32).astype(jnp.int32)
    slot_mine = jnp.sum(jnp.where(matches, ranks, 0), axis=0)
    return received.reshape(row_count * slot_count, lanes)[owner_mine * slot_count + slot_mine]


def exchange(orbitals, point_index, coulomb, fitting):
    my_row = lax.axis_index("row")
    my_col = lax.axis_index("col")
    height, core = my_col // 2, my_col % 2
    order = plane_order(my_row, my_col)
    strip = picked_strip(orbitals, point_index, my_row)

    column_pieces = gather_plane(to_plane(strip, 0))
    panel = strip.reshape((1,) + strip.shape)
    panel_pieces = gather_line(panel, swap_cores(panel), "z")
    place = jnp.array(REL, jnp.int32).repeat(2)
    cores = jnp.tile(jnp.array([0, 1], jnp.int32), SIDE)
    panel_order = jnp.concatenate(
        [((height + place) % SIDE) * 2 + (core ^ cores), jnp.stack([core, height])]
    ).astype(jnp.int32)
    keep, send = pair_weights(order, panel_order, column_pieces, panel_pieces, coulomb)

    summed = keep + swap_cores(send)
    parts = [to_plane(summed[turn], turn) for turn in range(SIDE)]
    w_strip = (parts[0] + parts[1]) + (parts[2] + parts[3])
    pieces = gather_plane(w_strip)

    def targets(*steps):
        chips = [(height + step) % SIDE for step in steps]
        return jnp.stack(chips + [core, core, core]).astype(jnp.int32)

    far_chips, own_chips = targets(2, -1, 1), targets(0, 1, -1)

    def both_cores(mine, other):
        other = swap_cores(other)
        return mine[0] + other[0], mine[1] + other[1]

    mine_far, other_far, mine, other, *weights = term(far_chips, fitting, gathered=(order, *pieces))
    far_low, far_high = both_cores(mine_far, other_far)
    far_up = move(far_low, "z", 1)
    far_down = move(far_high, "z", -1)
    down_low, up_high = both_cores(mine, other)
    after = (down_low, up_high)
    up_high = move(up_high, "z", 1)
    down_low = move(down_low, "z", -1)
    mine_own, other_own, mine, other = term(own_chips, fitting, weights=weights, after=after)
    up_low, down_high = both_cores(mine, other)
    up_low = move(up_low + far_up, "z", 1)
    down_high = move(down_high + far_down, "z", -1)
    own_low, own_high = both_cores(mine_own, other_own)
    low = own_low + (up_low + down_low)
    high = own_high + (up_high + down_high)
    return -jnp.concatenate([low, high], axis=0)


def solution(mesh):
    in_specs = (P("row", "col"), P(), P("row", "col"), P("row", "col"))
    out_specs = P("row", "col")
    return jax.shard_map(exchange, mesh=mesh, in_specs=in_specs, out_specs=out_specs, check_vma=False)
```

```python
import functools

import jax
import jax.numpy as jnp
from jax import lax
from jax.experimental import pallas as pl
from jax.experimental.pallas import tpu as pltpu
from jax.sharding import PartitionSpec as P


SIDE = 4
REL = (0, -1, 1, 2)
F32 = jnp.float32
BF16 = jnp.bfloat16


def shift(axis, step):
    pairs = []
    if axis == "z":
        for z in range(SIDE):
            for k in range(2):
                pairs.append((z * 2 + k, ((z + step) % SIDE) * 2 + k))
        return "col", pairs
    for y in range(SIDE):
        for x in range(SIDE):
            ty = (y + step) % SIDE if axis == "y" else y
            tx = (x + step) % SIDE if axis == "x" else x
            pairs.append((y * SIDE + x, ty * SIDE + tx))
    return "row", pairs


def move(value, axis, step):
    name, pairs = shift(axis, step)
    return lax.ppermute(value, name, pairs)


def swap_cores(value):
    return lax.ppermute(value, "col", [(c, c ^ 1) for c in range(2 * SIDE)])


def scatter_pairs(turn):
    pairs = []
    for y in range(SIDE):
        for x in range(SIDE):
            for z in range(SIDE):
                for k in range(2):
                    strip = (z + turn) % SIDE
                    ty = ((strip if k == 0 else -strip) - y) % SIDE
                    tx = x if k == 0 else x ^ 3
                    target = (ty * SIDE + tx) * 8 + y * 2 + (x >> 1)
                    pairs.append(((y * SIDE + x) * 8 + z * 2 + k, target))
    return pairs


def to_plane(value, turn):
    return lax.ppermute(value, ("row", "col"), scatter_pairs(turn))


def gather_line(low, high, axis):
    before_low, after_high = move(low, axis, 1), move(high, axis, -1)
    before_high, after_low = move(high, axis, 1), move(low, axis, -1)
    far_low, far_high = move(before_low, axis, 1), move(after_high, axis, -1)
    return low, high, before_low, before_high, after_low, after_high, far_low, far_high


def line_halves(block, axis):
    before, after, far = move(block, axis, 1), move(block, axis, -1), move(block, axis, 2)
    return jnp.stack([block, before]), jnp.stack([after, far])


def gather_plane(block):
    half = block.shape[0] // 2
    first = line_halves(block[:half], "x")
    second = line_halves(block[half:], "y")
    return gather_line(*first, "y") + gather_line(*second, "x")


def plane_order(my_row, my_col):
    rel = jnp.array(REL, jnp.int32)
    y, x = my_row // SIDE, my_row % SIDE
    z, k = my_col // 2, my_col % 2
    outer, inner = jnp.repeat(rel, SIDE), jnp.tile(rel, SIDE)

    def describe(dy, dx):
        py, px = (y + dy) % SIDE, (x + dx) % SIDE
        strip_k = (px >> 1) ^ k
        panel = (px & 1) ^ strip_k
        return panel, (jnp.where(strip_k == 0, py + z, -py - z) % SIDE) * 2 + strip_k

    first, second = describe(outer, inner), describe(inner, outer)
    return jnp.stack([first[0], first[1], second[0], second[1]])


def split(value):
    high = value.astype(BF16)
    return high, (value - high.astype(F32)).astype(BF16)


def dot3(a_high, a_low, b_high, b_low, dims):
    dot = functools.partial(
        lax.dot_general, dimension_numbers=(dims, ((), ())), preferred_element_type=F32
    )
    return dot(a_high, b_high) + (dot(a_high, b_low) + dot(a_low, b_high))


def piece_blocks(pieces):
    found, position = [], 0
    for ref in pieces:
        for block in range(ref.shape[0]):
            found.append((ref, block, position))
            position += 1
    return found


def pair_kernel(order, panel_order, chips, *refs):
    first, second, panels = refs[:8], refs[8:16], refs[16:24]
    coulomb_in, keep, send = refs[24:27]
    column, panel, p_high, p_low, c_high, c_low, t_high, t_low, total, coulomb, column_sem, panel_sem = refs[27:]
    rows = first[0].shape[1]
    lanes = first[0].shape[2]
    panel_copies = [pltpu.make_async_copy(coulomb_in, coulomb, panel_sem.at[8])]
    for ref, block, position in piece_blocks(panels):
        lane = pl.multiple_of(panel_order[position] * lanes, lanes)
        panel_copies.append(
            pltpu.make_async_copy(ref.at[block], panel.at[:, pl.ds(lane, lanes)], panel_sem.at[position])
        )
        panel_copies[-1].start()
    panel_copies[0].start()
    for which, pieces in enumerate((first, second)):
        for ref, block, position in piece_blocks(pieces):
            part = order[2 * which, position] * 2 + which
            strip = order[2 * which + 1, position]
            row = pl.multiple_of(part * rows, rows)
            lane = pl.multiple_of(strip * lanes, lanes)
            pltpu.make_async_copy(
                ref.at[block],
                column.at[pl.ds(row, rows), pl.ds(lane, lanes)],
                column_sem.at[part * 8 + strip],
            ).start()
    for copy in panel_copies:
        copy.wait()
    p_high[...], p_low[...] = split(panel[...])

    @pl.loop(0, 4)
    def _(step):
        part = lax.rem(step, 2) * 2 + step // 2
        here = pl.ds(pl.multiple_of(part * rows, rows), rows)
        for strip in range(8):
            pltpu.make_async_copy(
                first[0].at[0], column.at[here, pl.ds(strip * lanes, lanes)], column_sem.at[part * 8 + strip]
            ).wait()
        high, low = split(column[here, :])
        c_high[here, :], c_low[here, :] = high, low
        pair = dot3(p_high[...], p_low[...], high, low, ((1,), (1,)))
        t_high[:, here], t_low[:, here] = split(coulomb[:, here] * pair)

    @pl.loop(0, 4)
    def _(step):
        here = pl.ds(pl.multiple_of(step * 256, 256), 256)
        total[:, here] = dot3(t_high[...], t_low[...], c_high[:, here], c_low[:, here], ((1,), (0,)))

    core, height = chips[4], chips[3]
    count = keep.shape[1]
    for turn in range(SIDE):
        strip = lax.rem(height + turn, SIDE) * 2
        keep[turn] = total[pl.ds(pl.multiple_of((strip + core) * count, count), count), :]
        send[turn] = total[pl.ds(pl.multiple_of((strip + 1 - core) * count, count), count), :]


def pair_weights(order, panel_order, chips, column_pieces, panel_pieces, coulomb):
    rows, width = coulomb.shape
    bands = 8 * 128
    anywhere = pl.BlockSpec(memory_space=pl.ANY)
    scalars = pl.BlockSpec(memory_space=pltpu.SMEM)
    vmem = pl.BlockSpec(memory_space=pltpu.VMEM)
    out = jax.ShapeDtypeStruct((SIDE, rows // 8, bands), F32)
    return pl.pallas_call(
        pair_kernel,
        out_shape=(out, out),
        in_specs=[scalars, scalars, scalars] + [anywhere] * 24 + [pl.BlockSpec(memory_space=pltpu.HBM)],
        out_specs=(vmem, vmem),
        scratch_shapes=[
            pltpu.VMEM((width, bands), F32),
            pltpu.VMEM((rows, bands), F32),
            pltpu.VMEM((rows, bands), BF16),
            pltpu.VMEM((rows, bands), BF16),
            pltpu.VMEM((width, bands), BF16),
            pltpu.VMEM((width, bands), BF16),
            pltpu.VMEM((rows, width), BF16),
            pltpu.VMEM((rows, width), BF16),
            pltpu.VMEM((rows, bands), F32),
            pltpu.VMEM((rows, width), F32),
            pltpu.SemaphoreType.DMA((32,)),
            pltpu.SemaphoreType.DMA((9,)),
        ],
        compiler_params=pltpu.CompilerParams(vmem_limit_bytes=32 << 20),
        cost_estimate=pl.CostEstimate(flops=12 * rows * width * bands, bytes_accessed=12 << 20, transcendentals=0),
        name="pair_weights",
    )(order, panel_order, chips, *column_pieces, *panel_pieces, pltpu.with_memory_space_constraint(coulomb, pltpu.HBM))


def term_kernel(gathered, where, *refs):
    tile = pl.program_id(0)
    if gathered:
        order, first, second = refs[0], refs[1:9], refs[9:17]
        fitting, outs, high_out, low_out, high, low, whole, sem = refs[17], refs[18:22], *refs[22:]
        kept = [
            pltpu.make_async_copy(high, high_out, sem.at[32]),
            pltpu.make_async_copy(low, low_out, sem.at[33]),
        ]

        @pl.when(tile == 0)
        def _():
            rows = first[0].shape[1]
            copies = []
            for which, pieces in enumerate((first, second)):
                for ref, block, position in piece_blocks(pieces):
                    strip = order[2 * which, position] * 8 + order[2 * which + 1, position]
                    row = pl.multiple_of((strip * 2 + which) * rows, rows)
                    copies.append(
                        pltpu.make_async_copy(
                            ref.at[block], whole.at[pl.ds(row, rows), :], sem.at[which * 16 + position]
                        )
                    )
            for copy in copies:
                copy.start()
            for copy in copies:
                copy.wait()
            high[...], low[...] = split(whole[...])
            for copy in kept:
                copy.start()

        @pl.when(tile == pl.num_programs(0) - 1)
        def _():
            for copy in kept:
                copy.wait()
    else:
        fitting, weights, outs = refs[0], refs[1:5], refs[7:11]
    f_high, f_low = split(fitting[...])
    even = where[4] == 0
    half = outs[0].shape[2]
    for group in range(2):
        if gathered:
            start = chip_of(True, group, tile, where) * 2 * half
            here = pl.ds(pl.multiple_of(start, 2 * half), 2 * half)
            w_high, w_low = high[:, here], low[:, here]
        else:
            w_high, w_low = weights[2 * group][...], weights[2 * group + 1][...]
        product = dot3(f_high, f_low, w_high, w_low, ((1,), (0,)))
        lower, upper = product[:, :half], product[:, half:]
        outs[2 * group][0] = jnp.where(even, lower, upper)
        outs[2 * group + 1][0] = jnp.where(even, upper, lower)


def chip_of(gathered, group, tile, where):
    if group == 0:
        return where[0] if gathered else where[3]
    return jnp.where((tile < 2) == gathered, where[1], where[2])


def term(where, fitting, gathered=None, weights=None, after=None):
    rows, points = fitting.shape
    bands = 8 * 128
    tile = rows // 4
    anywhere = pl.BlockSpec(memory_space=pltpu.HBM)
    streamed = pl.BlockSpec((tile, points), lambda i, where: (i, 0))
    half = pl.BlockSpec((1, tile, bands // 8), lambda i, where: (i // 2, lax.rem(i, 2), 0))
    out = [jax.ShapeDtypeStruct((2, rows // 2, bands // 8), F32)] * 4
    out_specs = [half] * 4
    scratch = []
    if gathered is not None:
        in_specs = [pl.BlockSpec(memory_space=pltpu.SMEM)] + [anywhere] * 16 + [streamed]
        operands = (*gathered, fitting)
        out += [jax.ShapeDtypeStruct((points, bands), BF16)] * 2
        out_specs += [anywhere] * 2
        scratch = [pltpu.VMEM((points, bands), BF16)] * 2
        scratch += [pltpu.VMEM((points, bands), F32), pltpu.SemaphoreType.DMA((34,))]
    else:
        in_specs = [streamed]
        for group in range(2):
            chosen = pl.BlockSpec(
                (points, bands // SIDE), lambda i, where, group=group: (0, chip_of(False, group, i, where))
            )
            in_specs += [chosen, chosen]
        in_specs += [anywhere] * 2
        operands = (fitting, *weights, *weights, *after)
    return pl.pallas_call(
        functools.partial(term_kernel, gathered is not None),
        out_shape=out,
        grid_spec=pltpu.PrefetchScalarGridSpec(
            num_scalar_prefetch=1,
            grid=(rows // tile,),
            in_specs=in_specs,
            out_specs=out_specs,
            scratch_shapes=scratch,
        ),
        cost_estimate=pl.CostEstimate(
            flops=12 * rows * points * bands // SIDE, bytes_accessed=16 << 20, transcendentals=0
        ),
        name="term",
    )(where, *operands)


def picked_strip(orbitals, point_index, my_row):
    row_count = SIDE * SIDE
    slab_rows, lanes = orbitals.shape
    per_panel = point_index.shape[0] // row_count
    slot_count = 2 * per_panel // row_count
    owner = point_index // slab_rows
    owner_grid = owner.reshape(row_count, per_panel)
    local_grid = (point_index - owner * slab_rows).reshape(row_count, per_panel)
    spot = jnp.arange(per_panel)
    earlier = (spot[:, None] < spot[None, :]).astype(BF16)
    mine = owner_grid == my_row
    rank = jnp.dot(mine.astype(BF16), earlier, preferred_element_type=F32).astype(jnp.int32)
    chosen = mine[:, :, None] & (rank[:, :, None] == jnp.arange(slot_count)[None, None, :])
    source_row = jnp.sum(jnp.where(chosen, local_grid[:, :, None], 0), axis=1)
    outgoing = orbitals[source_row.reshape(-1)].reshape(row_count, slot_count, lanes)
    received = lax.all_to_all(outgoing, "row", split_axis=0, concat_axis=0, tiled=True)
    owner_mine = lax.dynamic_slice_in_dim(owner_grid, my_row, 1, 0)[0]
    matches = owner_mine[None, :] == jnp.arange(row_count)[:, None]
    ranks = jnp.dot(matches.astype(BF16), earlier, preferred_element_type=F32).astype(jnp.int32)
    slot_mine = jnp.sum(jnp.where(matches, ranks, 0), axis=0)
    return received.reshape(row_count * slot_count, lanes)[owner_mine * slot_count + slot_mine]


def exchange(orbitals, point_index, coulomb, fitting):
    my_row = lax.axis_index("row")
    my_col = lax.axis_index("col")
    height, core = my_col // 2, my_col % 2
    order = plane_order(my_row, my_col)
    strip = picked_strip(orbitals, point_index, my_row)

    column_pieces = gather_plane(to_plane(strip, 0))
    panel = strip.reshape((1,) + strip.shape)
    panel_pieces = gather_line(panel, swap_cores(panel), "z")
    chips = (height + jnp.array([2, -1, 1, 0], jnp.int32)) % SIDE
    chips = jnp.concatenate([chips, core[None]]).astype(jnp.int32)
    place = jnp.array(REL, jnp.int32).repeat(2)
    cores = jnp.tile(jnp.array([0, 1], jnp.int32), SIDE)
    panel_order = (((height + place) % SIDE) * 2 + (core ^ cores)).astype(jnp.int32)
    keep, send = pair_weights(order, panel_order, chips, column_pieces, panel_pieces, coulomb)

    summed = keep + swap_cores(send)
    parts = [to_plane(summed[turn], turn) for turn in range(SIDE)]
    w_strip = (parts[0] + parts[1]) + (parts[2] + parts[3])
    pieces = gather_plane(w_strip)

    def both_cores(mine, other):
        other = swap_cores(other)
        return mine[0] + other[0], mine[1] + other[1]

    mine_far, other_far, mine, other, *weights = term(chips, fitting, gathered=(order, *pieces))
    far_low, far_high = both_cores(mine_far, other_far)
    far_up = move(far_low, "z", 1)
    far_down = move(far_high, "z", -1)
    down_low, up_high = both_cores(mine, other)
    after = (down_low, up_high)
    up_high = move(up_high, "z", 1)
    down_low = move(down_low, "z", -1)
    mine_own, other_own, mine, other = term(chips, fitting, weights=weights, after=after)
    up_low, down_high = both_cores(mine, other)
    up_low = move(up_low + far_up, "z", 1)
    down_high = move(down_high + far_down, "z", -1)
    own_low, own_high = both_cores(mine_own, other_own)
    low = own_low + (up_low + down_low)
    high = own_high + (up_high + down_high)
    return -jnp.concatenate([low, high], axis=0)


def solution(mesh):
    in_specs = (P("row", "col"), P(), P("row", "col"), P("row", "col"))
    out_specs = P("row", "col")
    return jax.shard_map(exchange, mesh=mesh, in_specs=in_specs, out_specs=out_specs, check_vma=False)
```

```python
import functools

import jax
import jax.numpy as jnp
from jax import lax
from jax.experimental import pallas as pl
from jax.experimental.pallas import tpu as pltpu
from jax.sharding import PartitionSpec as P


SIDE = 4
REL = (0, -1, 1, 2)
F32 = jnp.float32
BF16 = jnp.bfloat16


def shift(axis, step):
    pairs = []
    if axis == "z":
        for z in range(SIDE):
            for k in range(2):
                pairs.append((z * 2 + k, ((z + step) % SIDE) * 2 + k))
        return "col", pairs
    for y in range(SIDE):
        for x in range(SIDE):
            ty = (y + step) % SIDE if axis == "y" else y
            tx = (x + step) % SIDE if axis == "x" else x
            pairs.append((y * SIDE + x, ty * SIDE + tx))
    return "row", pairs


def move(value, axis, step):
    name, pairs = shift(axis, step)
    return lax.ppermute(value, name, pairs)


def swap_cores(value):
    return lax.ppermute(value, "col", [(c, c ^ 1) for c in range(2 * SIDE)])


def scatter_pairs(turn):
    pairs = []
    for y in range(SIDE):
        for x in range(SIDE):
            for z in range(SIDE):
                for k in range(2):
                    strip = (z + turn) % SIDE
                    ty = (strip - y) % SIDE
                    tx = x if k == 0 else x ^ 3
                    target = (ty * SIDE + tx) * 8 + y * 2 + (x >> 1)
                    pairs.append(((y * SIDE + x) * 8 + z * 2 + k, target))
    return pairs


def to_plane(value, turn):
    return lax.ppermute(value, ("row", "col"), scatter_pairs(turn))


def gather_line(low, high, axis):
    before_low, after_high = move(low, axis, 1), move(high, axis, -1)
    before_high, after_low = move(high, axis, 1), move(low, axis, -1)
    far_low, far_high = move(before_low, axis, 1), move(after_high, axis, -1)
    return low, high, before_low, before_high, after_low, after_high, far_low, far_high


def line_halves(block, axis):
    before, after, far = move(block, axis, 1), move(block, axis, -1), move(block, axis, 2)
    return jnp.stack([block, before]), jnp.stack([after, far])


def gather_plane(block):
    half = block.shape[0] // 2
    first = line_halves(block[:half], "x")
    second = line_halves(block[half:], "y")
    return gather_line(*first, "y") + gather_line(*second, "x")


def plane_order(my_row, my_col):
    rel = jnp.array(REL, jnp.int32)
    y, x = my_row // SIDE, my_row % SIDE
    z, k = my_col // 2, my_col % 2
    outer, inner = jnp.repeat(rel, SIDE), jnp.tile(rel, SIDE)

    def describe(dy, dx):
        py, px = (y + dy) % SIDE, (x + dx) % SIDE
        strip_k = (px >> 1) ^ k
        panel = (px & 1) ^ strip_k
        return panel, ((py + z) % SIDE) * 2 + strip_k

    first, second = describe(outer, inner), describe(inner, outer)
    return jnp.stack([first[0], first[1], second[0], second[1]])


def split(value):
    high = value.astype(BF16)
    return high, (value - high.astype(F32)).astype(BF16)


def dot3(a_high, a_low, b_high, b_low, dims):
    dot = functools.partial(
        lax.dot_general, dimension_numbers=(dims, ((), ())), preferred_element_type=F32
    )
    return dot(a_high, b_high) + (dot(a_high, b_low) + dot(a_low, b_high))


def piece_blocks(pieces):
    found, position = [], 0
    for ref in pieces:
        for block in range(ref.shape[0]):
            found.append((ref, block, position))
            position += 1
    return found


def pair_kernel(order, panel_order, chips, *refs):
    first, second, panels = refs[:8], refs[8:16], refs[16:24]
    coulomb_in, keep, send = refs[24:27]
    column, panel, p_high, p_low, c_high, c_low, t_high, t_low, total, coulomb, column_sem, panel_sem = refs[27:]
    rows = first[0].shape[1]
    lanes = first[0].shape[2]
    panel_copies = [pltpu.make_async_copy(coulomb_in, coulomb, panel_sem.at[8])]
    for ref, block, position in piece_blocks(panels):
        lane = pl.multiple_of(panel_order[position] * lanes, lanes)
        panel_copies.append(
            pltpu.make_async_copy(ref.at[block], panel.at[:, pl.ds(lane, lanes)], panel_sem.at[position])
        )
        panel_copies[-1].start()
    panel_copies[0].start()
    for which, pieces in enumerate((first, second)):
        for ref, block, position in piece_blocks(pieces):
            part = order[2 * which, position] * 2 + which
            strip = order[2 * which + 1, position]
            row = pl.multiple_of(part * rows, rows)
            lane = pl.multiple_of(strip * lanes, lanes)
            pltpu.make_async_copy(
                ref.at[block],
                column.at[pl.ds(row, rows), pl.ds(lane, lanes)],
                column_sem.at[part * 8 + strip],
            ).start()
    for copy in panel_copies:
        copy.wait()
    p_high[...], p_low[...] = split(panel[...])

    @pl.loop(0, 4)
    def _(step):
        part = lax.rem(step, 2) * 2 + step // 2
        here = pl.ds(pl.multiple_of(part * rows, rows), rows)
        for strip in range(8):
            pltpu.make_async_copy(
                first[0].at[0], column.at[here, pl.ds(strip * lanes, lanes)], column_sem.at[part * 8 + strip]
            ).wait()
        high, low = split(column[here, :])
        c_high[here, :], c_low[here, :] = high, low
        pair = dot3(p_high[...], p_low[...], high, low, ((1,), (1,)))
        t_high[:, here], t_low[:, here] = split(coulomb[:, here] * pair)

    @pl.loop(0, 4)
    def _(step):
        here = pl.ds(pl.multiple_of(step * 256, 256), 256)
        total[:, here] = dot3(t_high[...], t_low[...], c_high[:, here], c_low[:, here], ((1,), (0,)))

    core, height = chips[4], chips[3]
    count = keep.shape[1]
    for turn in range(SIDE):
        strip = lax.rem(height + turn, SIDE) * 2
        keep[turn] = total[pl.ds(pl.multiple_of((strip + core) * count, count), count), :]
        send[turn] = total[pl.ds(pl.multiple_of((strip + 1 - core) * count, count), count), :]


def pair_weights(order, panel_order, chips, column_pieces, panel_pieces, coulomb):
    rows, width = coulomb.shape
    bands = 8 * 128
    anywhere = pl.BlockSpec(memory_space=pl.ANY)
    scalars = pl.BlockSpec(memory_space=pltpu.SMEM)
    vmem = pl.BlockSpec(memory_space=pltpu.VMEM)
    out = jax.ShapeDtypeStruct((SIDE, rows // 8, bands), F32)
    return pl.pallas_call(
        pair_kernel,
        out_shape=(out, out),
        in_specs=[scalars, scalars, scalars] + [anywhere] * 24 + [pl.BlockSpec(memory_space=pltpu.HBM)],
        out_specs=(vmem, vmem),
        scratch_shapes=[
            pltpu.VMEM((width, bands), F32),
            pltpu.VMEM((rows, bands), F32),
            pltpu.VMEM((rows, bands), BF16),
            pltpu.VMEM((rows, bands), BF16),
            pltpu.VMEM((width, bands), BF16),
            pltpu.VMEM((width, bands), BF16),
            pltpu.VMEM((rows, width), BF16),
            pltpu.VMEM((rows, width), BF16),
            pltpu.VMEM((rows, bands), F32),
            pltpu.VMEM((rows, width), F32),
            pltpu.SemaphoreType.DMA((32,)),
            pltpu.SemaphoreType.DMA((9,)),
        ],
        compiler_params=pltpu.CompilerParams(vmem_limit_bytes=32 << 20),
        cost_estimate=pl.CostEstimate(flops=12 * rows * width * bands, bytes_accessed=12 << 20, transcendentals=0),
        name="pair_weights",
    )(order, panel_order, chips, *column_pieces, *panel_pieces, pltpu.with_memory_space_constraint(coulomb, pltpu.HBM))


def term_kernel(gathered, where, *refs):
    tile = pl.program_id(0)
    if gathered:
        order, first, second = refs[0], refs[1:9], refs[9:17]
        fitting, outs, high_out, low_out, high, low, whole, sem = refs[17], refs[18:22], *refs[22:]
        kept = [
            pltpu.make_async_copy(high, high_out, sem.at[32]),
            pltpu.make_async_copy(low, low_out, sem.at[33]),
        ]

        @pl.when(tile == 0)
        def _():
            rows = first[0].shape[1]
            copies = []
            for which, pieces in enumerate((first, second)):
                for ref, block, position in piece_blocks(pieces):
                    strip = order[2 * which, position] * 8 + order[2 * which + 1, position]
                    row = pl.multiple_of((strip * 2 + which) * rows, rows)
                    copies.append(
                        pltpu.make_async_copy(
                            ref.at[block], whole.at[pl.ds(row, rows), :], sem.at[which * 16 + position]
                        )
                    )
            for copy in copies:
                copy.start()
            for copy in copies:
                copy.wait()
            high[...], low[...] = split(whole[...])
            for copy in kept:
                copy.start()

        @pl.when(tile == pl.num_programs(0) - 1)
        def _():
            for copy in kept:
                copy.wait()
    else:
        fitting, weights, outs = refs[0], refs[1:5], refs[7:11]
    f_high, f_low = split(fitting[...])
    even = where[4] == 0
    half = outs[0].shape[2]
    for group in range(2):
        if gathered:
            start = chip_of(True, group, tile, where) * 2 * half
            here = pl.ds(pl.multiple_of(start, 2 * half), 2 * half)
            w_high, w_low = high[:, here], low[:, here]
        else:
            w_high, w_low = weights[2 * group][...], weights[2 * group + 1][...]
        product = dot3(f_high, f_low, w_high, w_low, ((1,), (0,)))
        lower, upper = product[:, :half], product[:, half:]
        outs[2 * group][0] = jnp.where(even, lower, upper)
        outs[2 * group + 1][0] = jnp.where(even, upper, lower)


def chip_of(gathered, group, tile, where):
    if group == 0:
        return where[0] if gathered else where[3]
    return jnp.where((tile < 2) == gathered, where[1], where[2])


def term(where, fitting, gathered=None, weights=None, after=None):
    rows, points = fitting.shape
    bands = 8 * 128
    tile = rows // 4
    anywhere = pl.BlockSpec(memory_space=pltpu.HBM)
    streamed = pl.BlockSpec((tile, points), lambda i, where: (i, 0))
    half = pl.BlockSpec((1, tile, bands // 8), lambda i, where: (i // 2, lax.rem(i, 2), 0))
    out = [jax.ShapeDtypeStruct((2, rows // 2, bands // 8), F32)] * 4
    out_specs = [half] * 4
    scratch = []
    if gathered is not None:
        in_specs = [pl.BlockSpec(memory_space=pltpu.SMEM)] + [anywhere] * 16 + [streamed]
        operands = (*gathered, fitting)
        out += [jax.ShapeDtypeStruct((points, bands), BF16)] * 2
        out_specs += [anywhere] * 2
        scratch = [pltpu.VMEM((points, bands), BF16)] * 2
        scratch += [pltpu.VMEM((points, bands), F32), pltpu.SemaphoreType.DMA((34,))]
    else:
        in_specs = [streamed]
        for group in range(2):
            chosen = pl.BlockSpec(
                (points, bands // SIDE), lambda i, where, group=group: (0, chip_of(False, group, i, where))
            )
            in_specs += [chosen, chosen]
        in_specs += [pl.BlockSpec(memory_space=pl.ANY)] * 2
        operands = (fitting, *weights, *weights, *after)
    return pl.pallas_call(
        functools.partial(term_kernel, gathered is not None),
        out_shape=out,
        grid_spec=pltpu.PrefetchScalarGridSpec(
            num_scalar_prefetch=1,
            grid=(rows // tile,),
            in_specs=in_specs,
            out_specs=out_specs,
            scratch_shapes=scratch,
        ),
        cost_estimate=pl.CostEstimate(
            flops=12 * rows * points * bands // SIDE, bytes_accessed=16 << 20, transcendentals=0
        ),
        name="term",
    )(where, *operands)


def picked_strip(orbitals, point_index, my_row):
    row_count = SIDE * SIDE
    slab_rows, lanes = orbitals.shape
    per_panel = point_index.shape[0] // row_count
    slot_count = 2 * per_panel // row_count
    owner = point_index // slab_rows
    owner_grid = owner.reshape(row_count, per_panel)
    local_grid = (point_index - owner * slab_rows).reshape(row_count, per_panel)
    spot = jnp.arange(per_panel)
    earlier = (spot[:, None] < spot[None, :]).astype(BF16)
    mine = owner_grid == my_row
    rank = jnp.dot(mine.astype(BF16), earlier, preferred_element_type=F32).astype(jnp.int32)
    chosen = mine[:, :, None] & (rank[:, :, None] == jnp.arange(slot_count)[None, None, :])
    source_row = jnp.sum(jnp.where(chosen, local_grid[:, :, None], 0), axis=1)
    outgoing = orbitals[source_row.reshape(-1)].reshape(row_count, slot_count, lanes)
    received = lax.all_to_all(outgoing, "row", split_axis=0, concat_axis=0, tiled=True)
    owner_mine = lax.dynamic_slice_in_dim(owner_grid, my_row, 1, 0)[0]
    matches = owner_mine[None, :] == jnp.arange(row_count)[:, None]
    ranks = jnp.dot(matches.astype(BF16), earlier, preferred_element_type=F32).astype(jnp.int32)
    slot_mine = jnp.sum(jnp.where(matches, ranks, 0), axis=0)
    return received.reshape(row_count * slot_count, lanes)[owner_mine * slot_count + slot_mine]


def exchange(orbitals, point_index, coulomb, fitting):
    my_row = lax.axis_index("row")
    my_col = lax.axis_index("col")
    height, core = my_col // 2, my_col % 2
    order = plane_order(my_row, my_col)
    strip = picked_strip(orbitals, point_index, my_row)

    column_pieces = gather_plane(to_plane(strip, 0))
    panel = strip.reshape((1,) + strip.shape)
    panel_pieces = gather_line(panel, swap_cores(panel), "z")
    chips = (height + jnp.array([2, -1, 1, 0], jnp.int32)) % SIDE
    chips = jnp.concatenate([chips, core[None]]).astype(jnp.int32)
    place = jnp.array(REL, jnp.int32).repeat(2)
    cores = jnp.tile(jnp.array([0, 1], jnp.int32), SIDE)
    panel_order = (((height + place) % SIDE) * 2 + (core ^ cores)).astype(jnp.int32)
    keep, send = pair_weights(order, panel_order, chips, column_pieces, panel_pieces, coulomb)

    summed = keep + swap_cores(send)
    parts = [to_plane(summed[turn], turn) for turn in range(SIDE)]
    w_strip = (parts[0] + parts[1]) + (parts[2] + parts[3])
    pieces = gather_plane(w_strip)

    def both_cores(mine, other):
        other = swap_cores(other)
        return mine[0] + other[0], mine[1] + other[1]

    mine_far, other_far, mine, other, *weights = term(chips, fitting, gathered=(order, *pieces))
    far_low, far_high = both_cores(mine_far, other_far)
    far_up = move(far_low, "z", 1)
    far_down = move(far_high, "z", -1)
    down_low, up_high = both_cores(mine, other)
    after = (down_low, up_high)
    up_high = move(up_high, "z", 1)
    down_low = move(down_low, "z", -1)
    mine_own, other_own, mine, other = term(chips, fitting, weights=weights, after=after)
    up_low, down_high = both_cores(mine, other)
    up_low = move(up_low + far_up, "z", 1)
    down_high = move(down_high + far_down, "z", -1)
    own_low, own_high = both_cores(mine_own, other_own)
    low = own_low + (up_low + down_low)
    high = own_high + (up_high + down_high)
    return -jnp.concatenate([low, high], axis=0)


def solution(mesh):
    in_specs = (P("row", "col"), P(), P("row", "col"), P("row", "col"))
    out_specs = P("row", "col")
    return jax.shard_map(exchange, mesh=mesh, in_specs=in_specs, out_specs=out_specs, check_vma=False)
```
